32 devices in a mesh: phys: 4 (over y, x), row: 2 (over core), col: 4 (over z).
Axes of the slice: x: 2, y: 2, z: 4, core: 2. Of those that a mesh axis runs over, the one named last changes fastest.
Arguments:
- rho_sites: bfloat16 [1, 16, 2048, 2048], P(None, 'phys', 'row', 'col'), may hold values from -0.0625 to 0.0625
- sigma_sites: bfloat16 [1, 16, 2048, 2048], P(None, 'phys', 'row', 'col'), may hold values from -0.0625 to 0.0625
- environment: float32 [2048, 2048], P('row', 'col'), may hold values from -6 to 6
Outputs:
- new_environment: float32 [2048, 2048], P('row', 'col')
The draws below stay inside these ranges and needn't reach their ends.
All inputs are finite; a program needn't handle non-finite values.
Results may differ from the reference program's by a relative error of at most 0.004.
Values may be sent and summed in bfloat16 or wider, within the bound.
A program may use at most 128 MiB of HBM per device.

```python
import jax
import jax.numpy as jnp

CHI = 2048
PAIRS = 16
SITES = 1


def shard_levels(own_key, shape, split, low, high):
    level = 1.0
    for position, shards_of in split:
        heights = jax.random.uniform(jax.random.fold_in(jax.random.fold_in(own_key, 6), position), (shards_of,), jnp.float32, low / len(split), high / len(split))
        level = level * jnp.repeat(jnp.exp(heights), shape[position] // shards_of).reshape((-1,) + (1,) * (len(shape) - 1 - position))
    return level


def bell_draw(key, shape, width, limit, split=(), dtype=jnp.bfloat16):
    values = width * jax.random.normal(key, shape, jnp.float32)
    if split:
        values = values * shard_levels(key, shape, split, -0.22, 0.18)
    return jnp.clip(values, -limit, limit).astype(dtype)


def setup_inputs(seed: int = 0) -> dict:
    key_of = jax.random.split(jax.random.key(seed), 4)
    rho_sites = bell_draw(key_of[0], (SITES, PAIRS, CHI, CHI), (4 * CHI) ** -0.5, 0.0625, ((1, 4), (2, 2), (3, 4)))
    sigma_sites = bell_draw(key_of[1], (SITES, PAIRS, CHI, CHI), (4 * CHI) ** -0.5, 0.0625, ((1, 4), (2, 2), (3, 4)))
    environment = bell_draw(key_of[2], (CHI, CHI), 1.0, 6.0, ((0, 2), (1, 4)), jnp.float32)
    return {"rho_sites": rho_sites, "sigma_sites": sigma_sites, "environment": environment}


def reference(rho_sites, sigma_sites, environment):
    env = environment
    for site in range(SITES):
        env_b = env.astype(jnp.bfloat16)
        total = jnp.zeros((CHI, CHI), jnp.float32)
        for pair in range(PAIRS):
            half = jnp.dot(env_b, sigma_sites[site, pair], preferred_element_type=jnp.float32).astype(jnp.bfloat16)
            total = total + jnp.dot(rho_sites[site, pair].T, half, preferred_element_type=jnp.float32)
        env = total
    return env
```

```python
import functools

import jax
import jax.numpy as jnp
from jax import lax
from jax.experimental import pallas as pl
from jax.experimental.pallas import tpu as pltpu
from jax.sharding import PartitionSpec as P

MESH = pl.DeviceIdType.MESH
NCH = 4
FROM_RIGHT = {
    0: [("r", 1, k) for k in range(4)] + [("r", 2, k) for k in range(3)] + [None],
    1: [("r", 2, 0), ("r", 2, 1), ("r", 2, 2), ("r", 3, 0), ("r", 3, 1), ("r", 3, 2), ("r", 3, 3), ("r", 2, 3)],
    2: [("r", 3, k) for k in range(4)] + [("h", p) for p in range(4)],
    3: [None] * 8,
}


def mirror(item):
    if item is None or item[0] == "h":
        return item
    return ("r", 3 - item[1], item[2])


FROM_LEFT = {3 - c: [mirror(i) for i in seq] for c, seq in FROM_RIGHT.items()}
PASS_LEFT = {
    (2, 1): [(3, 0)], (2, 2): [(3, 1)], (2, 3): [(3, 2)], (2, 4): [(3, 3), (2, 3)],
    (1, 1): [(2, 0)], (1, 2): [(2, 1)], (1, 3): [(2, 2)],
}
PASS_RIGHT = {(3 - c, t): [(3 - b, k) for b, k in v] for (c, t), v in PASS_LEFT.items()}
FIRST_LEFT = {1: [(1, k) for k in range(4)], 2: [(2, 0), (2, 1), (2, 2)], 3: [(3, k) for k in range(4)]}
FIRST_RIGHT = {3 - c: [(3 - b, k) for b, k in v] for c, v in FIRST_LEFT.items()}
FOR_END = [(3, 0), (3, 1), (3, 2), (3, 3), (2, 3)]
NREM = len(FOR_END)
F32 = jnp.float32
BF16 = jnp.bfloat16


def kernel(rho_ref, sig_ref, env_ref, out_ref,
           rho_g, sig, env_f, env_g, half, half_r, acc, psend, rbuf, s1, f1, s2, f2,
           rl_send, rr_send, r_recv, l_send, l_recv, h_send, h_recv, loc, sg_send, sg_recv,
           el_send, er_send, e_recv, ex_send, ex_recv, ey_send, ey_recv,
           row_send, row_recv, x_send, x_recv, y_send, y_recv, z_send, z_recv):
    ph = lax.axis_index("phys")
    r = lax.axis_index("row")
    c = lax.axis_index("col")
    width = rho_g.shape[-1]
    rows = rho_g.shape[3]
    quarter = rows // 4
    ind3 = c // 3
    ind2 = c // 2 - ind3
    ind0 = (3 - c) // 3
    ind1 = 1 - ind0 - ind2 - ind3
    inds = (ind0, ind1, ind2, ind3)

    def pick(values):
        total = 0
        for i, v in zip(inds, values):
            total = total + i * v
        return total

    mate = {"row": 1 - r}
    xn = {"phys": ph + 1 - 2 * (ph % 2)}
    yn = {"phys": (ph + 2) % 4}
    left = {"col": c - 1}
    right = {"col": c + 1}
    mid = jnp.logical_and(c > 0, c < 3)
    middle = {"col": 3 - c}
    end = {"col": 3 * (c // 2)}

    def remote(src, dst, ss, rs, dev):
        return pltpu.make_async_remote_copy(src_ref=src, dst_ref=dst, send_sem=ss, recv_sem=rs,
                                            device_id=dev, device_id_type=MESH)

    load_env = pltpu.make_async_copy(env_ref, env_f, loc.at[0])
    load_env.start()
    load_rho = [pltpu.make_async_copy(rho_ref.at[0, :, :, pl.ds(k * width, width)], rho_g.at[c, k], loc.at[1 + k]) for k in range(NCH)]
    for cp in load_rho:
        cp.start()
    my_rows = pl.ds(pl.multiple_of(r * rows, rows), rows)
    load_sig = pltpu.make_async_copy(sig_ref.at[0], sig.at[:, my_rows, :], loc.at[1 + NCH])
    load_sig.start()

    barrier = pltpu.get_barrier_semaphore()
    for dev in (mate, xn, yn):
        pl.semaphore_signal(barrier, inc=1, device_id=dev, device_id_type=MESH)

    @pl.when(c > 0)
    def _():
        pl.semaphore_signal(barrier, inc=1, device_id=left, device_id_type=MESH)

    @pl.when(c < 3)
    def _():
        pl.semaphore_signal(barrier, inc=1, device_id=right, device_id_type=MESH)

    load_env.wait()
    env_g[c] = env_f[...].astype(BF16)
    pl.semaphore_wait(barrier, 3 + pick((1, 2, 2, 1)))

    q_rows = pl.ds(pl.multiple_of(ph * quarter, quarter), quarter)
    h_rows = pl.ds(pl.multiple_of((ph // 2) * 2 * quarter, 2 * quarter), 2 * quarter)

    def env_left(b):
        return remote(env_g.at[b, q_rows], env_g.at[b, q_rows], el_send.at[b], e_recv.at[b], left)

    def env_right(b):
        return remote(env_g.at[b, q_rows], env_g.at[b, q_rows], er_send.at[b], e_recv.at[b], right)

    def env_x(b):
        return remote(env_g.at[b, q_rows], env_g.at[b, q_rows], ex_send.at[b], ex_recv.at[b], xn)

    def env_y(b):
        return remote(env_g.at[b, h_rows], env_g.at[b, h_rows], ey_send.at[b], ey_recv.at[b], yn)

    def send_left(b, k):
        return remote(rho_g.at[b, k], rho_g.at[b, k], rl_send.at[b, k], r_recv.at[b, k], left)

    def send_right(b, k):
        return remote(rho_g.at[b, k], rho_g.at[b, k], rr_send.at[b, k], r_recv.at[b, k], right)

    def first_piece(p):
        at = rho_g.at[c, 0, p]
        remote(at, at, rl_send.at[c, 0], r_recv.at[c, 0], left).start()
        remote(at, at, rr_send.at[c, 0], r_recv.at[c, 0], right).start()

    def last_piece(b, p):
        return remote(rho_g.at[b, NCH - 1, p], rho_g.at[b, NCH - 1, p], l_send.at[p], l_recv.at[p], middle)

    @pl.when(c > 0)
    def _():
        env_left(c).start()

    @pl.when(c < 3)
    def _():
        env_right(c).start()

    give_sig = remote(sig_ref.at[0], sig.at[:, my_rows, :], sg_send, sg_recv, mate)
    load_rho[0].wait()

    @pl.when(mid)
    def _():
        first_piece(0)
    give_sig.start()

    def first_sends(i, k):
        for b, kk in FIRST_LEFT.get(i, []):
            if kk == k:
                send_left(b, k).start()
        for b, kk in FIRST_RIGHT.get(i, []):
            if kk == k:
                send_right(b, k).start()

    for k in range(NCH):
        if k:
            load_rho[k].wait()
        for i in (0, 3):
            @pl.when(c == i)
            def _():
                first_sends(i, k)

    for d in range(1, 4):
        @pl.when(c >= d)
        def _(b=c - d):
            env_right(b).wait_recv()

            @pl.when(c < 3)
            def _():
                env_right(b).start()
            env_x(b).start()

        @pl.when(c + d <= 3)
        def _(b=c + d):
            env_left(b).wait_recv()

            @pl.when(c > 0)
            def _():
                env_left(b).start()
            env_x(b).start()
        if d == 1:
            @pl.when(mid)
            def _():
                first_piece(1)
        if d == 2:
            @pl.when(mid)
            def _():
                first_piece(2)
                first_piece(3)
            for i in (1, 2):
                @pl.when(c == i)
                def _():
                    for k in range(1, NCH):
                        first_sends(i, k)

    def others(f):
        for d in range(1, 4):
            @pl.when(c >= d)
            def _(b=c - d):
                f(b)

            @pl.when(c + d <= 3)
            def _(b=c + d):
                f(b)

    def env_y_of(b):
        env_x(b).wait_recv()
        env_y(b).start()
    others(env_y_of)
    others(lambda b: env_y(b).wait_recv())
    load_sig.wait()
    give_sig.wait_recv()

    tile = min(256, rows)

    @pl.loop(0, 4)
    def _(p):
        @pl.loop(0, rows // tile)
        def _(m):
            here = pl.ds(pl.multiple_of(m * tile, tile), tile)
            total = jnp.dot(env_g[0, here, :], sig[p, pl.ds(0, 512), :], preferred_element_type=F32)
            for b in range(1, 4):
                total += jnp.dot(env_g[b, here, :], sig[p, pl.ds(b * 512, 512), :], preferred_element_type=F32)
            half[p, here, :] = total.astype(BF16)

    def unit_of(b, k):
        return (b % 2) * NCH + k

    def product(b, k, other, unit, first=0, last=4):
        if first == 0:
            acc[unit] = jnp.zeros_like(acc.at[unit])

        @pl.loop(first, last)
        def _(p):
            acc[unit] += lax.dot_general(rho_g[b, k, p], other[p], (((0,), (0,)), ((), ())),
                                         preferred_element_type=F32)

    part_a = pl.ds(0, width // 2)
    part_b = pl.ds(width // 2, width // 2)

    def row_copy(unit):
        return remote(psend.at[unit], rbuf.at[unit], row_send.at[unit], row_recv.at[unit], mate)

    def one_x(u):
        return remote(s1.at[u, part_a], f1.at[u, part_a], x_send.at[u, 0], x_recv.at[u, 0], xn)

    def one_y(u):
        return remote(s1.at[u, part_b], f1.at[u, part_b], y_send.at[u, 0], y_recv.at[u, 0], yn)

    def two_y(u):
        return remote(s2.at[u, part_a], f2.at[u, part_a], y_send.at[u, 1], y_recv.at[u, 1], yn)

    def two_x(u):
        return remote(s2.at[u, part_b], f2.at[u, part_b], x_send.at[u, 1], x_recv.at[u, 1], xn)

    def end_chunk(q):
        b, k = FOR_END[q]
        return pick((0, b, 3 - b, 0)), k

    def end_unit(q):
        b, k = FOR_END[q]
        there, mirrored = unit_of(b, k), unit_of(3 - b, k)
        return pick((there, there, mirrored, mirrored))

    def z_copy(q):
        return remote(s1.at[2 * NCH + q], s1.at[end_unit(q)], z_send.at[q], z_recv.at[q], end)

    def unit_at(pos):
        _, b, k, q = pos
        return unit_of(b, k) if q is None else 2 * NCH + q

    def slot_at(pos):
        _, b, k, q = pos
        if q is not None:
            return 2 * NCH + q
        owner = b // 2
        own = 1 - (owner + r - 2 * owner * r)
        return own * unit_of(b, k) + (1 - own) * (2 * NCH + NREM)

    def to_mate(pos):
        @pl.when(pos[1] // 2 != r)
        def _():
            psend[unit_at(pos)] = acc[slot_at(pos)].astype(BF16)
            row_copy(unit_at(pos)).start()

    def stage0(pos, first=0):
        valid, b, k, q = pos

        @pl.when(valid)
        def _():
            product(b, k, half if q is None else half_r, slot_at(pos), first)
            to_mate(pos)

    def owned(pos, f):
        valid, b, k, q = pos

        @pl.when(jnp.logical_and(valid, b // 2 == r))
        def _():
            f(unit_at(pos))

    def begin(u):
        one_x(u).start()
        one_y(u).start()

    def turn(u):
        one_x(u).wait_recv()
        s2[u, part_a] = (s1[u, part_a].astype(F32) + f1[u, part_a].astype(F32)).astype(BF16)
        two_y(u).start()
        one_y(u).wait_recv()
        s2[u, part_b] = (s1[u, part_b].astype(F32) + f1[u, part_b].astype(F32)).astype(BF16)
        two_x(u).start()

    def finish(u):
        two_y(u).wait_recv()
        two_x(u).wait_recv()
        at = pl.ds(pl.multiple_of(u * width, width), width)
        out_ref[at, :] = s2[u].astype(F32) + f2[u].astype(F32)

    def stage1(pos):
        def f(unit):
            row_copy(unit).wait_recv()
            s1[unit] = (acc[unit] + rbuf[unit].astype(F32)).astype(BF16)
            if pos[3] is None:
                begin(unit)
            else:
                z_copy(pos[3]).start()
        owned(pos, f)

    line = []

    def advance(pos):
        if pos is not None:
            stage0(pos)
        line.append(pos)
        n = len(line) - 1
        if n >= 2 and line[n - 2] is not None:
            stage1(line[n - 2])
        if n >= 4 and line[n - 4] is not None:
            owned(line[n - 4], turn)
        if n >= 6 and line[n - 6] is not None:
            owned(line[n - 6], finish)

    def half_copy(p, dev):
        return remote(half.at[p], half_r.at[p], h_send.at[p], h_recv.at[p], dev)

    true = c >= 0

    def arrive(t):
        for i in range(4):
            @pl.when(c == i)
            def _():
                for table, passed, send in ((FROM_RIGHT, PASS_LEFT, send_left), (FROM_LEFT, PASS_RIGHT, send_right)):
                    item = table[i][t - 1]
                    if item is None:
                        continue
                    if item[0] == "h":
                        half_copy(item[1], left if i == 2 else right).wait_recv()
                    else:
                        send(item[1], item[2]).wait_recv()
                    for b, k in passed.get((i, t), []):
                        if b == i:
                            for p in range(4):
                                last_piece(c, p).start()
                        else:
                            send(b, k).start()

    def positions(t):
        for table in (FROM_RIGHT, FROM_LEFT):
            items = [table[i][t - 1] for i in range(4)]
            ok = [1 if it is not None and it[0] == "r" else 0 for it in items]
            blocks = [it[1] if o else 0 for it, o in zip(items, ok)]
            chunks = [it[2] if o else 0 for it, o in zip(items, ok)]
            yield (pick(ok) == 1, pick(blocks), pick(chunks), None)

    def for_end(q):
        return (mid,) + end_chunk(q) + (q,)

    def part_for_end(q, first, last):
        @pl.when(mid)
        def _():
            product(*end_chunk(q), half_r, 2 * NCH + q, first, last)

    early = {5: [(0, 0, 1), (1, 0, 1)], 6: [(0, 1, 2), (1, 1, 2), (2, 0, 2)],
             7: [(0, 2, 3), (1, 2, 3), (2, 2, 3), (3, 0, 3)]}
    arrive(1)
    for k in range(NCH):
        advance((true, c, k, None))

    @pl.when(c == 0)
    def _():
        for p in range(4):
            half_copy(p, right).start()

    @pl.when(c == 3)
    def _():
        for p in range(4):
            half_copy(p, left).start()

    for t in range(1, 8):
        if t > 1:
            arrive(t)
        for pos in positions(t):
            advance(pos)
        for q, first, last in early.get(t, []):
            part_for_end(q, first, last)
    for _ in range(6):
        advance(None)

    own_last = (mid, 3 - c, NCH - 1, None)
    end_last = for_end(NREM - 1)

    def last_products(p):
        last_piece(3 - c, p).wait_recv()
        product(3 - c, NCH - 1, half_r, slot_at(end_last), p, p + 1)
        if p == 3:
            to_mate(end_last)
        product(3 - c, NCH - 1, half, slot_at(own_last), p, p + 1)
        if p == 3:
            to_mate(own_last)

    @pl.when(mid)
    def _():
        last_products(0)
        last_products(1)
        half_copy(3, middle).wait_recv()
        for q in range(NREM - 1):
            stage0(for_end(q), 3)
        for q in range(NREM - 1):
            stage1(for_end(q))
        last_products(2)
        last_products(3)
        stage1(end_last)
        stage1(own_last)
        owned(own_last, turn)
        owned(own_last, finish)

    keeper = jnp.logical_or(jnp.logical_and(c == 0, r == 1), jnp.logical_and(c == 3, r == 0))

    @pl.when(keeper)
    def _():
        for step, q in (("z", 0), ("z", 1), ("t", 0), ("z", 2), ("t", 1), ("f", 0), ("z", 3), ("t", 2), ("f", 1),
                        ("t", 3), ("z", 4), ("f", 2), ("f", 3), ("t", 4), ("f", 4)):
            if step == "z":
                z_copy(q).wait_recv()
                begin(end_unit(q))
            elif step == "t":
                turn(end_unit(q))
            else:
                finish(end_unit(q))

    give_sig.wait_send()

    @pl.when(c > 0)
    def _():
        env_left(c).wait_send()

    @pl.when(c < 3)
    def _():
        env_right(c).wait_send()
    for d in range(1, 4):
        @pl.when(c >= d)
        def _(b=c - d):
            @pl.when(c < 3)
            def _():
                env_right(b).wait_send()
            env_x(b).wait_send()
            env_y(b).wait_send()

        @pl.when(c + d <= 3)
        def _(b=c + d):
            @pl.when(c > 0)
            def _():
                env_left(b).wait_send()
            env_x(b).wait_send()
            env_y(b).wait_send()
    for i in range(4):
        @pl.when(c == i)
        def _():
            for first, passed, send in ((FIRST_LEFT, PASS_LEFT, send_left), (FIRST_RIGHT, PASS_RIGHT, send_right)):
                todo = list(first.get(i, []))
                for (j, t), v in passed.items():
                    if j == i:
                        todo += [(b, k) for b, k in v if b != i]
                for b, k in todo:
                    send(b, k).wait_send()
            if i in (0, 3):
                for p in range(4):
                    half_copy(p, right if i == 0 else left).wait_send()
            else:
                for p in range(4):
                    last_piece(c, p).wait_send()

    def exchanged(u):
        one_x(u).wait_send()
        one_y(u).wait_send()
        two_y(u).wait_send()
        two_x(u).wait_send()

    for pos in [pos for pos in line if pos is not None] + [own_last] + [for_end(q) for q in range(NREM)]:
        @pl.when(pos[0])
        def _():
            unit = unit_at(pos)

            @pl.when(pos[1] // 2 != r)
            def _():
                row_copy(unit).wait_send()

            @pl.when(pos[1] // 2 == r)
            def _():
                if pos[3] is None:
                    exchanged(unit)
                else:
                    z_copy(pos[3]).wait_send()

    @pl.when(keeper)
    def _():
        for q in range(NREM):
            exchanged(end_unit(q))


def fused(rho_sites, sigma_sites, environment):
    _, pairs, rows, cols = rho_sites.shape
    width = cols // NCH
    units = 2 * NCH
    sem = pltpu.SemaphoreType.DMA
    piece = (units + NREM, width, cols)
    pair = (units, width, cols)
    return pl.pallas_call(
        kernel,
        out_shape=pltpu.VMEM(environment.shape, F32),
        in_specs=[pl.BlockSpec(memory_space=pl.ANY)] * 3,
        out_specs=pl.BlockSpec(memory_space=pltpu.VMEM),
        scratch_shapes=[
            pltpu.VMEM((4, NCH, pairs, rows, width), BF16),
            pltpu.VMEM((pairs, 2 * rows, cols), BF16),
            pltpu.VMEM((rows, cols), F32),
            pltpu.VMEM((4, rows, cols), BF16),
            pltpu.VMEM((pairs, rows, cols), BF16),
            pltpu.VMEM((pairs, rows, cols), BF16),
            pltpu.VMEM((units + NREM + 1, width, cols), F32),
            pltpu.VMEM(piece, BF16), pltpu.VMEM(piece, BF16), pltpu.VMEM(piece, BF16),
            pltpu.VMEM(pair, BF16), pltpu.VMEM(pair, BF16), pltpu.VMEM(pair, BF16),
            sem((4, NCH)), sem((4, NCH)), sem((4, NCH)), sem((4,)), sem((4,)), sem((4,)), sem((4,)),
            sem((2 + NCH,)), sem, sem,
            sem((4,)), sem((4,)), sem((4,)), sem((4,)), sem((4,)), sem((4,)), sem((4,)),
            sem((units + NREM,)), sem((units + NREM,)),
            sem((units, 2)), sem((units, 2)), sem((units, 2)), sem((units, 2)),
            sem((NREM,)), sem((NREM,)),
        ],
        compiler_params=pltpu.CompilerParams(
            collective_id=0, has_side_effects=True, vmem_limit_bytes=58 * 1024 * 1024
        ),
    )(rho_sites, sigma_sites, environment)


def plain(rho_sites, sigma_sites, environment):
    env_whole = lax.all_gather(environment.astype(BF16), "col", axis=1, tiled=True)
    half = jnp.einsum(
        "ik,pkl->pil",
        env_whole,
        lax.all_gather(sigma_sites[0], "row", axis=1, tiled=True),
        preferred_element_type=F32,
    ).astype(BF16)
    partial_env = jnp.einsum(
        "pij,pil->jl",
        lax.all_gather(rho_sites[0], "col", axis=2, tiled=True),
        half,
        preferred_element_type=F32,
    )
    row_part = lax.psum_scatter(partial_env, "row", scatter_dimension=0, tiled=True)
    return lax.psum(row_part, "phys")


def solution(mesh):
    placed = (P(None, "phys", "row", "col"), P(None, "phys", "row", "col"), P("row", "col"))
    sizes = (mesh.shape["phys"], mesh.shape["row"], mesh.shape["col"])
    body = fused if sizes == (4, 2, 4) else plain
    return jax.shard_map(body, mesh=mesh, in_specs=placed, out_specs=P("row", "col"), check_vma=False)
```

```python
import functools

import jax
import jax.numpy as jnp
from jax import lax
from jax.experimental import pallas as pl
from jax.experimental.pallas import tpu as pltpu
from jax.sharding import PartitionSpec as P

MESH = pl.DeviceIdType.MESH
NCH = 4
FROM_RIGHT = {
    0: [("r", 1, k) for k in range(4)] + [None] * 3,
    1: [("r", 2, 0), ("r", 2, 1), ("r", 2, 2), ("r", 3, 0), ("r", 3, 1), ("r", 3, 2), ("r", 3, 3)],
    2: [("r", 3, k) for k in range(4)] + [("h", p) for p in range(3)],
    3: [None] * 7,
}


def mirror(item):
    if item is None or item[0] == "h":
        return item
    return ("r", 3 - item[1], item[2])


FROM_LEFT = {3 - c: [mirror(i) for i in seq] for c, seq in FROM_RIGHT.items()}
PASS_LEFT = {(2, 1): [(3, 0)], (2, 2): [(3, 1)], (2, 3): [(3, 2)], (2, 4): [(3, 3), (2, 3)]}
PASS_RIGHT = {(3 - c, t): [(3 - b, k) for b, k in v] for (c, t), v in PASS_LEFT.items()}
FIRST_LEFT = {1: [(1, k) for k in range(4)], 2: [(2, 0), (2, 1), (2, 2)], 3: [(3, k) for k in range(4)]}
FIRST_RIGHT = {3 - c: [(3 - b, k) for b, k in v] for c, v in FIRST_LEFT.items()}
FOR_END = [(2, 0), (2, 1), (2, 2), (3, 0), (3, 1), (3, 2), (3, 3), (2, 3)]
NREM = len(FOR_END)
SPLIT = 3
LAST_ORDER = (3, 0, 1, 2)
F32 = jnp.float32
BF16 = jnp.bfloat16


def kernel(rho_ref, sig_ref, env_ref, out_ref,
           rho_g, sig, env_f, env_g, half, half_r, acc, psend, rbuf, s1, f1, s2, f2, zbuf,
           rl_send, rr_send, r_recv, l_send, l_recv, h_send, h_recv, loc, sg_send, sg_recv,
           el_send, er_send, e_recv, ex_send, ex_recv, ey_send, ey_recv,
           row_send, row_recv, x_send, x_recv, y_send, y_recv, z_send, z_recv):
    ph = lax.axis_index("phys")
    r = lax.axis_index("row")
    c = lax.axis_index("col")
    width = rho_g.shape[-1]
    rows = rho_g.shape[3]
    quarter = rows // 4
    ind3 = c // 3
    ind2 = c // 2 - ind3
    ind0 = (3 - c) // 3
    ind1 = 1 - ind0 - ind2 - ind3
    inds = (ind0, ind1, ind2, ind3)

    def pick(values):
        total = 0
        for i, v in zip(inds, values):
            total = total + i * v
        return total

    mate = {"row": 1 - r}
    xn = {"phys": ph + 1 - 2 * (ph % 2)}
    yn = {"phys": (ph + 2) % 4}
    left = {"col": c - 1}
    right = {"col": c + 1}
    mid = jnp.logical_and(c > 0, c < 3)
    middle = {"col": 3 - c}
    end = {"col": 3 * (c // 2)}

    def remote(src, dst, ss, rs, dev):
        return pltpu.make_async_remote_copy(src_ref=src, dst_ref=dst, send_sem=ss, recv_sem=rs,
                                            device_id=dev, device_id_type=MESH)

    load_env = pltpu.make_async_copy(env_ref, env_f, loc.at[0])
    load_env.start()
    load_rho = [pltpu.make_async_copy(rho_ref.at[0, :, :, pl.ds(k * width, width)], rho_g.at[c, k], loc.at[1 + k]) for k in range(NCH)]
    for cp in load_rho:
        cp.start()
    my_rows = pl.ds(pl.multiple_of(r * rows, rows), rows)
    load_sig = pltpu.make_async_copy(sig_ref.at[0], sig.at[:, my_rows, :], loc.at[1 + NCH])
    load_sig.start()

    barrier = pltpu.get_barrier_semaphore()
    for dev in (mate, xn, yn):
        pl.semaphore_signal(barrier, inc=1, device_id=dev, device_id_type=MESH)

    @pl.when(c > 0)
    def _():
        pl.semaphore_signal(barrier, inc=1, device_id=left, device_id_type=MESH)

    @pl.when(c < 3)
    def _():
        pl.semaphore_signal(barrier, inc=1, device_id=right, device_id_type=MESH)

    load_env.wait()
    env_g[c] = env_f[...].astype(BF16)
    pl.semaphore_wait(barrier, 3 + pick((1, 2, 2, 1)))

    q_rows = pl.ds(pl.multiple_of(ph * quarter, quarter), quarter)
    h_rows = pl.ds(pl.multiple_of((ph // 2) * 2 * quarter, 2 * quarter), 2 * quarter)

    def env_left(b):
        return remote(env_g.at[b, q_rows], env_g.at[b, q_rows], el_send.at[b], e_recv.at[b], left)

    def env_right(b):
        return remote(env_g.at[b, q_rows], env_g.at[b, q_rows], er_send.at[b], e_recv.at[b], right)

    def env_x(b):
        return remote(env_g.at[b, q_rows], env_g.at[b, q_rows], ex_send.at[b], ex_recv.at[b], xn)

    def env_y(b):
        return remote(env_g.at[b, h_rows], env_g.at[b, h_rows], ey_send.at[b], ey_recv.at[b], yn)

    def send_left(b, k):
        return remote(rho_g.at[b, k], rho_g.at[b, k], rl_send.at[b, k], r_recv.at[b, k], left)

    def send_right(b, k):
        return remote(rho_g.at[b, k], rho_g.at[b, k], rr_send.at[b, k], r_recv.at[b, k], right)

    def first_piece(p):
        at = rho_g.at[c, 0, p]
        remote(at, at, rl_send.at[c, 0], r_recv.at[c, 0], left).start()
        remote(at, at, rr_send.at[c, 0], r_recv.at[c, 0], right).start()

    def pass_piece(b, k, dev):
        at = rho_g.at[b, k, SPLIT]
        return remote(at, at, rl_send.at[b, k], r_recv.at[b, k], dev)

    def last_piece(b, p):
        return remote(rho_g.at[b, NCH - 1, p], rho_g.at[b, NCH - 1, p], l_send.at[p], l_recv.at[p], middle)

    @pl.when(c > 0)
    def _():
        env_left(c).start()

    @pl.when(c < 3)
    def _():
        env_right(c).start()

    give_sig = remote(sig_ref.at[0], sig.at[:, my_rows, :], sg_send, sg_recv, mate)
    load_rho[0].wait()

    @pl.when(mid)
    def _():
        first_piece(0)
    give_sig.start()

    def first_sends(i, k):
        for b, kk in FIRST_LEFT.get(i, []):
            if kk == k:
                send_left(b, k).start()
        for b, kk in FIRST_RIGHT.get(i, []):
            if kk == k:
                send_right(b, k).start()

    for k in range(NCH):
        if k:
            load_rho[k].wait()
        for i in (0, 3):
            @pl.when(c == i)
            def _():
                first_sends(i, k)

    for d in range(1, 4):
        @pl.when(c >= d)
        def _(b=c - d):
            env_right(b).wait_recv()

            @pl.when(c < 3)
            def _():
                env_right(b).start()
            env_x(b).start()

        @pl.when(c + d <= 3)
        def _(b=c + d):
            env_left(b).wait_recv()

            @pl.when(c > 0)
            def _():
                env_left(b).start()
            env_x(b).start()
        if d == 1:
            @pl.when(mid)
            def _():
                first_piece(1)
        if d == 2:
            @pl.when(mid)
            def _():
                first_piece(2)
                first_piece(3)
            for i in (1, 2):
                @pl.when(c == i)
                def _():
                    for k in range(1, NCH):
                        first_sends(i, k)

    def others(f):
        for d in range(1, 4):
            @pl.when(c >= d)
            def _(b=c - d):
                f(b)

            @pl.when(c + d <= 3)
            def _(b=c + d):
                f(b)

    def env_y_of(b):
        env_x(b).wait_recv()
        env_y(b).start()
    others(env_y_of)
    others(lambda b: env_y(b).wait_recv())
    load_sig.wait()
    give_sig.wait_recv()

    tile = min(256, rows)

    @pl.loop(0, 4)
    def _(p):
        @pl.loop(0, rows // tile)
        def _(m):
            here = pl.ds(pl.multiple_of(m * tile, tile), tile)
            total = jnp.dot(env_g[0, here, :], sig[p, pl.ds(0, 512), :], preferred_element_type=F32)
            for b in range(1, 4):
                total += jnp.dot(env_g[b, here, :], sig[p, pl.ds(b * 512, 512), :], preferred_element_type=F32)
            half[p, here, :] = total.astype(BF16)

    def unit_of(b, k):
        return (b % 2) * NCH + k

    def product(b, k, other, unit, first=0, last=4, zero=None):
        if zero or (zero is None and first == 0):
            acc[unit] = jnp.zeros_like(acc.at[unit])

        @pl.loop(first, last)
        def _(p):
            acc[unit] += lax.dot_general(rho_g[b, k, p], other[p], (((0,), (0,)), ((), ())),
                                         preferred_element_type=F32)

    part_a = pl.ds(0, width // 2)
    part_b = pl.ds(width // 2, width // 2)

    def row_copy(unit):
        return remote(psend.at[unit], rbuf.at[unit], row_send.at[unit], row_recv.at[unit], mate)

    def one_x(u):
        return remote(s1.at[u, part_a], f1.at[u, part_a], x_send.at[u, 0], x_recv.at[u, 0], xn)

    def one_y(u):
        return remote(s1.at[u, part_b], f1.at[u, part_b], y_send.at[u, 0], y_recv.at[u, 0], yn)

    def two_y(u):
        return remote(s2.at[u, part_a], f2.at[u, part_a], y_send.at[u, 1], y_recv.at[u, 1], yn)

    def two_x(u):
        return remote(s2.at[u, part_b], f2.at[u, part_b], x_send.at[u, 1], x_recv.at[u, 1], xn)

    def end_chunk(q):
        b, k = FOR_END[q]
        return pick((b, b, 3 - b, 3 - b)), k

    def end_unit(q):
        b, k = FOR_END[q]
        there, mirrored = unit_of(b, k), unit_of(3 - b, k)
        return pick((there, there, mirrored, mirrored))

    def z_copy(q):
        return remote(s1.at[2 * NCH + q], zbuf.at[end_unit(q)], z_send.at[q], z_recv.at[q], end)

    def end_piece(q):
        return pass_piece(*end_chunk(q), end)

    def unit_at(pos):
        _, b, k, q = pos
        return unit_of(b, k) if q is None else 2 * NCH + q

    def slot_at(pos):
        _, b, k, q = pos
        if q is not None:
            return 2 * NCH + q
        owner = b // 2
        own = 1 - (owner + r - 2 * owner * r)
        return own * unit_of(b, k) + (1 - own) * (2 * NCH + NREM)

    def to_mate(pos):
        @pl.when(pos[1] // 2 != r)
        def _():
            psend[unit_at(pos)] = acc[slot_at(pos)].astype(BF16)
            row_copy(unit_at(pos)).start()

    def stage0(pos, first=0):
        valid, b, k, q = pos

        @pl.when(valid)
        def _():
            product(b, k, half if q is None else half_r, slot_at(pos), first)
            to_mate(pos)

    def owned(pos, f):
        valid, b, k, q = pos

        @pl.when(jnp.logical_and(valid, b // 2 == r))
        def _():
            f(unit_at(pos))

    def begin(u):
        one_x(u).start()
        one_y(u).start()

    def turn(u):
        one_x(u).wait_recv()
        s2[u, part_a] = (s1[u, part_a].astype(F32) + f1[u, part_a].astype(F32)).astype(BF16)
        two_y(u).start()
        one_y(u).wait_recv()
        s2[u, part_b] = (s1[u, part_b].astype(F32) + f1[u, part_b].astype(F32)).astype(BF16)
        two_x(u).start()

    def finish(u):
        two_y(u).wait_recv()
        two_x(u).wait_recv()
        at = pl.ds(pl.multiple_of(u * width, width), width)
        out_ref[at, :] = s2[u].astype(F32) + f2[u].astype(F32)

    def stage1(pos):
        def f(unit):
            row_copy(unit).wait_recv()
            s1[unit] = (acc[unit] + rbuf[unit].astype(F32)).astype(BF16)
            if pos[3] is None:
                begin(unit)
            else:
                z_copy(pos[3]).start()
        owned(pos, f)

    line = []

    def advance(pos):
        if pos is not None:
            stage0(pos)
        line.append(pos)
        n = len(line) - 1
        if n >= 2 and line[n - 2] is not None:
            stage1(line[n - 2])
        if n >= 4 and line[n - 4] is not None:
            owned(line[n - 4], turn)
        if n >= 6 and line[n - 6] is not None:
            owned(line[n - 6], finish)

    def half_copy(p, dev):
        return remote(half.at[p], half_r.at[p], h_send.at[p], h_recv.at[p], dev)

    true = c >= 0

    def arrive(t, kinds="rh"):
        for i in range(4):
            @pl.when(c == i)
            def _():
                for table, passed, send, on in ((FROM_RIGHT, PASS_LEFT, send_left, 1), (FROM_LEFT, PASS_RIGHT, send_right, 2)):
                    item = table[i][t - 1]
                    if item is None or item[0] not in kinds:
                        continue
                    if item[0] == "h":
                        half_copy(item[1], left if i == 2 else right).wait_recv()
                    else:
                        send(item[1], item[2]).wait_recv()
                        if i == on:
                            pass_piece(item[1], item[2], end).start()
                        for b, k in passed.get((i, t), []):
                            if b == i:
                                for p in LAST_ORDER:
                                    last_piece(c, p).start()
                            else:
                                send(b, k).start()

    def for_end(q):
        return (mid,) + end_chunk(q) + (q,)

    def part_for_end(q, first, last):
        @pl.when(mid)
        def _():
            product(*end_chunk(q), half_r, 2 * NCH + q, first, last)

    def positions(t):
        for table in (FROM_RIGHT, FROM_LEFT):
            items = [table[i][t - 1] for i in range(4)]
            ok = [1 if it is not None and it[0] == "r" else 0 for it in items]
            blocks = [it[1] if o else 0 for it, o in zip(items, ok)]
            chunks = [it[2] if o else 0 for it, o in zip(items, ok)]
            yield (pick(ok) == 1, pick(blocks), pick(chunks), None)

    arrive(1)
    for k in range(NCH):
        advance((true, c, k, None))

    @pl.when(c == 0)
    def _():
        for p in range(SPLIT):
            half_copy(p, right).start()

    @pl.when(c == 3)
    def _():
        for p in range(SPLIT):
            half_copy(p, left).start()

    for t in range(1, 7):
        if t > 1:
            arrive(t)
        for pos in positions(t):
            advance(pos)
        if t == 5:
            for q in range(5):
                part_for_end(q, 0, 1)
        if t == 6:
            for q in range(5):
                part_for_end(q, 1, 2)
            part_for_end(5, 0, 2)
    arrive(7, "h")

    @pl.when(mid)
    def _():
        for q in range(6):
            product(*end_chunk(q), half_r, 2 * NCH + q, 2, 3)
            to_mate(for_end(q))
        for q in range(6):
            stage1(for_end(q))
    arrive(7, "r")
    for pos in positions(7):
        advance(pos)

    @pl.when(mid)
    def _():
        product(*end_chunk(6), half_r, 2 * NCH + 6, 0, 3)
        to_mate(for_end(6))
        stage1(for_end(6))
    for _ in range(6):
        advance(None)

    own_last = (mid, 3 - c, NCH - 1, None)
    end_last = for_end(NREM - 1)
    at_end = jnp.logical_or(c == 0, c == 3)
    keeper = jnp.logical_or(jnp.logical_and(c == 0, r == 1), jnp.logical_and(c == 3, r == 0))

    def exchanged(u):
        one_x(u).wait_send()
        one_y(u).wait_send()
        two_y(u).wait_send()
        two_x(u).wait_send()

    def sent(pos):
        @pl.when(pos[0])
        def _():
            unit = unit_at(pos)

            @pl.when(pos[1] // 2 != r)
            def _():
                row_copy(unit).wait_send()

            @pl.when(pos[1] // 2 == r)
            def _():
                if pos[3] is None:
                    exchanged(unit)
                else:
                    z_copy(pos[3]).wait_send()

    def settle():
        give_sig.wait_send()

        @pl.when(c > 0)
        def _():
            env_left(c).wait_send()

        @pl.when(c < 3)
        def _():
            env_right(c).wait_send()
        for d in range(1, 4):
            @pl.when(c >= d)
            def _(b=c - d):
                @pl.when(c < 3)
                def _():
                    env_right(b).wait_send()
                env_x(b).wait_send()
                env_y(b).wait_send()

            @pl.when(c + d <= 3)
            def _(b=c + d):
                @pl.when(c > 0)
                def _():
                    env_left(b).wait_send()
                env_x(b).wait_send()
                env_y(b).wait_send()
        for i in range(4):
            @pl.when(c == i)
            def _():
                for first, passed, send in ((FIRST_LEFT, PASS_LEFT, send_left), (FIRST_RIGHT, PASS_RIGHT, send_right)):
                    todo = list(first.get(i, []))
                    for (j, t), v in passed.items():
                        if j == i:
                            todo += [(b, k) for b, k in v if b != i]
                    for b, k in todo:
                        send(b, k).wait_send()
                if i in (0, 3):
                    for p in range(SPLIT):
                        half_copy(p, right if i == 0 else left).wait_send()
        for pos in line:
            if pos is not None:
                sent(pos)

    @pl.when(mid)
    def _():
        settle()

    def last_products(p):
        last_piece(3 - c, p).wait_recv()
        first, final = p == LAST_ORDER[0], p == LAST_ORDER[-1]
        if p == SPLIT:
            end_piece(NREM - 1).start()
        else:
            product(3 - c, NCH - 1, half_r, slot_at(end_last), p, p + 1)
        if final:
            to_mate(end_last)
        product(3 - c, NCH - 1, half, slot_at(own_last), p, p + 1, zero=first)
        if final:
            to_mate(own_last)

    @pl.when(mid)
    def _():
        for q in range(6):
            end_piece(q).wait_send()
            sent(for_end(q))
        for p in LAST_ORDER:
            last_products(p)
        stage1(end_last)
        stage1(own_last)
        owned(own_last, turn)
        owned(own_last, finish)
        end_piece(6).wait_send()
        end_piece(7).wait_send()
        sent(for_end(6))
        sent(end_last)
        sent(own_last)
        for p in LAST_ORDER:
            last_piece(c, p).wait_send()

    def end_part(q):
        pos = (at_end,) + end_chunk(q) + (None,)
        end_piece(q).wait_recv()
        product(pos[1], pos[2], half, slot_at(pos), SPLIT, SPLIT + 1, zero=True)
        to_mate(pos)

    def gather(q):
        u = end_unit(q)
        row_copy(u).wait_recv()
        z_copy(q).wait_recv()
        s1[u] = (acc[u] + rbuf[u].astype(F32) + zbuf[u].astype(F32)).astype(BF16)
        begin(u)

    @pl.when(at_end)
    def _():
        for q in range(NREM - 2):
            end_part(q)
        settle()

        @pl.when(keeper)
        def _():
            for n in range(NREM - 2 + 4):
                if n < NREM - 2:
                    gather(n)
                if 0 <= n - 2 < NREM - 2:
                    turn(end_unit(n - 2))
                if 0 <= n - 4:
                    finish(end_unit(n - 4))
            for q in range(NREM - 2):
                exchanged(end_unit(q))
        for q in (NREM - 2, NREM - 1):
            end_part(q)

        @pl.when(keeper)
        def _():
            for q in (NREM - 2, NREM - 1):
                gather(q)
                turn(end_unit(q))
                finish(end_unit(q))
            for q in (NREM - 2, NREM - 1):
                exchanged(end_unit(q))

        @pl.when(jnp.logical_not(keeper))
        def _():
            for q in range(NREM):
                row_copy(end_unit(q)).wait_send()


def fused(rho_sites, sigma_sites, environment):
    _, pairs, rows, cols = rho_sites.shape
    width = cols // NCH
    units = 2 * NCH
    sem = pltpu.SemaphoreType.DMA
    piece = (units + NREM, width, cols)
    pair = (units, width, cols)
    return pl.pallas_call(
        kernel,
        out_shape=pltpu.VMEM(environment.shape, F32),
        in_specs=[pl.BlockSpec(memory_space=pl.ANY)] * 3,
        out_specs=pl.BlockSpec(memory_space=pltpu.VMEM),
        scratch_shapes=[
            pltpu.VMEM((4, NCH, pairs, rows, width), BF16),
            pltpu.VMEM((pairs, 2 * rows, cols), BF16),
            pltpu.VMEM((rows, cols), F32),
            pltpu.VMEM((4, rows, cols), BF16),
            pltpu.VMEM((pairs, rows, cols), BF16),
            pltpu.VMEM((pairs, rows, cols), BF16),
            pltpu.VMEM((units + NREM + 1, width, cols), F32),
            pltpu.VMEM(piece, BF16), pltpu.VMEM(piece, BF16), pltpu.VMEM(piece, BF16),
            pltpu.VMEM(pair, BF16), pltpu.VMEM(pair, BF16), pltpu.VMEM(pair, BF16), pltpu.VMEM(pair, BF16),
            sem((4, NCH)), sem((4, NCH)), sem((4, NCH)), sem((4,)), sem((4,)), sem((4,)), sem((4,)),
            sem((2 + NCH,)), sem, sem,
            sem((4,)), sem((4,)), sem((4,)), sem((4,)), sem((4,)), sem((4,)), sem((4,)),
            sem((units + NREM,)), sem((units + NREM,)),
            sem((units, 2)), sem((units, 2)), sem((units, 2)), sem((units, 2)),
            sem((NREM,)), sem((NREM,)),
        ],
        compiler_params=pltpu.CompilerParams(
            collective_id=0, has_side_effects=True, vmem_limit_bytes=58 * 1024 * 1024
        ),
    )(rho_sites, sigma_sites, environment)


def plain(rho_sites, sigma_sites, environment):
    env_whole = lax.all_gather(environment.astype(BF16), "col", axis=1, tiled=True)
    half = jnp.einsum(
        "ik,pkl->pil",
        env_whole,
        lax.all_gather(sigma_sites[0], "row", axis=1, tiled=True),
        preferred_element_type=F32,
    ).astype(BF16)
    partial_env = jnp.einsum(
        "pij,pil->jl",
        lax.all_gather(rho_sites[0], "col", axis=2, tiled=True),
        half,
        preferred_element_type=F32,
    )
    row_part = lax.psum_scatter(partial_env, "row", scatter_dimension=0, tiled=True)
    return lax.psum(row_part, "phys")


def solution(mesh):
    placed = (P(None, "phys", "row", "col"), P(None, "phys", "row", "col"), P("row", "col"))
    sizes = (mesh.shape["phys"], mesh.shape["row"], mesh.shape["col"])
    body = fused if sizes == (4, 2, 4) else plain
    return jax.shard_map(body, mesh=mesh, in_specs=placed, out_specs=P("row", "col"), check_vma=False)
```

```python
import functools

import jax
import jax.numpy as jnp
from jax import lax
from jax.experimental import pallas as pl
from jax.experimental.pallas import tpu as pltpu
from jax.sharding import PartitionSpec as P

MESH = pl.DeviceIdType.MESH
NCH = 4
FROM_RIGHT = {
    0: [("r", 1, k) for k in range(4)] + [None] * 3,
    1: [("r", 2, 0), ("r", 2, 1), ("r", 2, 2), ("r", 3, 0), ("r", 3, 1), ("r", 3, 2), ("r", 3, 3)],
    2: [("r", 3, k) for k in range(4)] + [("h", p) for p in range(3)],
    3: [None] * 7,
}


def mirror(item):
    if item is None or item[0] == "h":
        return item
    return ("r", 3 - item[1], item[2])


FROM_LEFT = {3 - c: [mirror(i) for i in seq] for c, seq in FROM_RIGHT.items()}
PASS_LEFT = {(2, 1): [(3, 0)], (2, 2): [(3, 1)], (2, 3): [(3, 2)], (2, 4): [(3, 3), (2, 3)]}
PASS_RIGHT = {(3 - c, t): [(3 - b, k) for b, k in v] for (c, t), v in PASS_LEFT.items()}
FIRST_LEFT = {1: [(1, k) for k in range(4)], 2: [(2, 0), (2, 1), (2, 2)], 3: [(3, k) for k in range(4)]}
FIRST_RIGHT = {3 - c: [(3 - b, k) for b, k in v] for c, v in FIRST_LEFT.items()}
FOR_END = [(2, 0), (2, 1), (2, 2), (3, 0), (3, 1), (3, 2), (3, 3), (2, 3)]
NREM = len(FOR_END)
SPLIT = 3
LAST_ORDER = (3, 0, 1, 2)
F32 = jnp.float32
BF16 = jnp.bfloat16


def kernel(rho_ref, sig_ref, env_ref, out_ref,
           rho_g, sig, env_f, env_g, half, half_r, acc, psend, rbuf, s1, f1, s2, f2, zbuf,
           r_send, r_recv, p_send, l_recv, h_recv, loc, sg_send, sg_recv,
           e_send, e_recv, ex_send, ex_recv, ey_send, ey_recv,
           row_send, row_recv, t_send, t_recv, u_recv):
    ph = lax.axis_index("phys")
    r = lax.axis_index("row")
    c = lax.axis_index("col")
    width = rho_g.shape[-1]
    rows = rho_g.shape[3]
    quarter = rows // 4
    ind3 = c // 3
    ind2 = c // 2 - ind3
    ind0 = (3 - c) // 3
    ind1 = 1 - ind0 - ind2 - ind3
    inds = (ind0, ind1, ind2, ind3)

    def pick(values):
        total = 0
        for i, v in zip(inds, values):
            total = total + i * v
        return total

    mate = {"row": 1 - r}
    xn = {"phys": ph + 1 - 2 * (ph % 2)}
    yn = {"phys": (ph + 2) % 4}
    left = {"col": c - 1}
    right = {"col": c + 1}
    mid = jnp.logical_and(c > 0, c < 3)
    middle = {"col": 3 - c}
    end = {"col": 3 * (c // 2)}

    def remote(src, dst, ss, rs, dev):
        return pltpu.make_async_remote_copy(src_ref=src, dst_ref=dst, send_sem=ss, recv_sem=rs,
                                            device_id=dev, device_id_type=MESH)

    env_parts = [pl.ds(pl.multiple_of((ph + j) % 4 * quarter, quarter), quarter) for j in range(4)]
    load_env = [pltpu.make_async_copy(env_ref.at[at], env_f.at[at], loc.at[1 + NCH + j]) for j, at in enumerate(env_parts)]
    load_env[0].start()
    load_rho = [pltpu.make_async_copy(rho_ref.at[0, :, :, pl.ds(k * width, width)], rho_g.at[c, k], loc.at[k]) for k in range(NCH)]
    for cp in load_rho:
        cp.start()
    for cp in load_env[1:]:
        cp.start()
    my_rows = pl.ds(pl.multiple_of(r * rows, rows), rows)
    load_sig = pltpu.make_async_copy(sig_ref.at[0], sig.at[:, my_rows, :], loc.at[NCH])
    load_sig.start()

    barrier = pltpu.get_barrier_semaphore()
    for dev in (mate, xn, yn):
        pl.semaphore_signal(barrier, inc=1, device_id=dev, device_id_type=MESH)

    @pl.when(c > 0)
    def _():
        pl.semaphore_signal(barrier, inc=1, device_id=left, device_id_type=MESH)

    @pl.when(c < 3)
    def _():
        pl.semaphore_signal(barrier, inc=1, device_id=right, device_id_type=MESH)

    def cast_env(j):
        load_env[j].wait()
        env_g[c, env_parts[j]] = env_f[env_parts[j]].astype(BF16)

    cast_env(0)
    pl.semaphore_wait(barrier, 3 + pick((1, 2, 2, 1)))

    q_rows = env_parts[0]
    h_rows = pl.ds(pl.multiple_of((ph // 2) * 2 * quarter, 2 * quarter), 2 * quarter)

    def env_left(b):
        return remote(env_g.at[b, q_rows], env_g.at[b, q_rows], e_send.at[b], e_recv.at[b], left)

    def env_right(b, slot=None):
        slot = b if slot is None else slot
        return remote(env_g.at[b, q_rows], env_g.at[b, q_rows], e_send.at[slot], e_recv.at[b], right)

    def env_x(b):
        return remote(env_g.at[b, q_rows], env_g.at[b, q_rows], ex_send.at[b], ex_recv.at[b], xn)

    def env_y(b):
        return remote(env_g.at[b, h_rows], env_g.at[b, h_rows], ey_send.at[b], ey_recv.at[b], yn)

    def send_left(b, k):
        return remote(rho_g.at[b, k], rho_g.at[b, k], r_send.at[b, k], r_recv.at[b, k], left)

    def send_right(b, k, slot=None):
        slot = b if slot is None else slot
        return remote(rho_g.at[b, k], rho_g.at[b, k], r_send.at[slot, k], r_recv.at[b, k], right)

    def first_piece(p):
        at = rho_g.at[c, 0, p]
        remote(at, at, r_send.at[c, 0], r_recv.at[c, 0], left).start()
        remote(at, at, r_send.at[4, 0], r_recv.at[c, 0], right).start()

    def pass_piece(b, k, dev):
        at = rho_g.at[b, k, SPLIT]
        return remote(at, at, r_send.at[b, k], r_recv.at[b, k], dev)

    def last_piece(b, p):
        return remote(rho_g.at[b, NCH - 1, p], rho_g.at[b, NCH - 1, p], p_send.at[p], l_recv.at[p], middle)

    @pl.when(c > 0)
    def _():
        env_left(c).start()

    @pl.when(c < 3)
    def _():
        env_right(c, 4).start()

    give_sig = remote(sig_ref.at[0], sig.at[:, my_rows, :], sg_send, sg_recv, mate)
    load_rho[0].wait()

    @pl.when(mid)
    def _():
        first_piece(0)
    give_sig.start()
    for j in range(1, 4):
        cast_env(j)

    def first_sends(i, k):
        for b, kk in FIRST_LEFT.get(i, []):
            if kk == k:
                send_left(b, k).start()
        for b, kk in FIRST_RIGHT.get(i, []):
            if kk == k:
                send_right(b, k, 4).start()

    for k in range(NCH):
        if k:
            load_rho[k].wait()
        for i in (0, 3):
            @pl.when(c == i)
            def _():
                first_sends(i, k)

    for d in range(1, 4):
        @pl.when(c >= d)
        def _(b=c - d):
            env_right(b).wait_recv()

            @pl.when(c < 3)
            def _():
                env_right(b).start()
            env_x(b).start()

        @pl.when(c + d <= 3)
        def _(b=c + d):
            env_left(b).wait_recv()

            @pl.when(c > 0)
            def _():
                env_left(b).start()
            env_x(b).start()
        if d == 1:
            @pl.when(mid)
            def _():
                first_piece(1)
        if d == 2:
            @pl.when(mid)
            def _():
                first_piece(2)
                first_piece(3)
            for i in (1, 2):
                @pl.when(c == i)
                def _():
                    for k in range(1, NCH):
                        first_sends(i, k)

    def others(f):
        for d in range(1, 4):
            @pl.when(c >= d)
            def _(b=c - d):
                f(b)

            @pl.when(c + d <= 3)
            def _(b=c + d):
                f(b)

    def env_y_of(b):
        env_x(b).wait_recv()
        env_y(b).start()
    others(env_y_of)
    others(lambda b: env_y(b).wait_recv())
    load_sig.wait()
    give_sig.wait_recv()

    tile = min(256, rows)

    @pl.loop(0, 4)
    def _(p):
        @pl.loop(0, rows // tile)
        def _(m):
            here = pl.ds(pl.multiple_of(m * tile, tile), tile)
            total = jnp.dot(env_g[0, here, :], sig[p, pl.ds(0, 512), :], preferred_element_type=F32)
            for b in range(1, 4):
                total += jnp.dot(env_g[b, here, :], sig[p, pl.ds(b * 512, 512), :], preferred_element_type=F32)
            half[p, here, :] = total.astype(BF16)

    def unit_of(b, k):
        return (b % 2) * NCH + k

    def product(b, k, other, unit, first=0, last=4, zero=None):
        if zero or (zero is None and first == 0):
            acc[unit] = jnp.zeros_like(acc.at[unit])

        @pl.loop(first, last)
        def _(p):
            acc[unit] += lax.dot_general(rho_g[b, k, p], other[p], (((0,), (0,)), ((), ())),
                                         preferred_element_type=F32)

    part_a = pl.ds(0, width // 2)
    part_b = pl.ds(width // 2, width // 2)

    def row_copy(unit):
        return remote(psend.at[unit], rbuf.at[unit], row_send.at[unit], row_recv.at[unit], mate)

    def one_x(u):
        return remote(s1.at[u, part_a], f1.at[u, part_a], t_send.at[u], t_recv.at[u], xn)

    def one_y(u):
        return remote(s1.at[u, part_b], f1.at[u, part_b], t_send.at[u], t_recv.at[u], yn)

    def two_y(u):
        return remote(s2.at[u, part_a], f2.at[u, part_a], t_send.at[u], u_recv.at[u], yn)

    def two_x(u):
        return remote(s2.at[u, part_b], f2.at[u, part_b], t_send.at[u], u_recv.at[u], xn)

    def end_chunk(q):
        b, k = FOR_END[q]
        return pick((b, b, 3 - b, 3 - b)), k

    def end_unit(q):
        b, k = FOR_END[q]
        there, mirrored = unit_of(b, k), unit_of(3 - b, k)
        return pick((there, there, mirrored, mirrored))

    def z_copy(q):
        return remote(s1.at[2 * NCH + q], zbuf.at[end_unit(q)], row_send.at[2 * NCH + q], row_recv.at[2 * NCH + q], end)

    def end_piece(q):
        return pass_piece(*end_chunk(q), end)

    def unit_at(pos):
        _, b, k, q = pos
        return unit_of(b, k) if q is None else 2 * NCH + q

    def slot_at(pos):
        _, b, k, q = pos
        if q is not None:
            return 2 * NCH + q
        owner = b // 2
        own = 1 - (owner + r - 2 * owner * r)
        return own * unit_of(b, k) + (1 - own) * (2 * NCH + NREM)

    def to_mate(pos):
        @pl.when(pos[1] // 2 != r)
        def _():
            psend[unit_at(pos)] = acc[slot_at(pos)].astype(BF16)
            row_copy(unit_at(pos)).start()

    def stage0(pos, first=0):
        valid, b, k, q = pos

        @pl.when(valid)
        def _():
            product(b, k, half if q is None else half_r, slot_at(pos), first)
            to_mate(pos)

    def owned(pos, f):
        valid, b, k, q = pos

        @pl.when(jnp.logical_and(valid, b // 2 == r))
        def _():
            f(unit_at(pos))

    def begin(u):
        one_x(u).start()
        one_y(u).start()

    def turn(u):
        remote(s1.at[u], f1.at[u], t_send.at[u], t_recv.at[u], xn).wait_recv()
        s2[u, part_a] = (s1[u, part_a].astype(F32) + f1[u, part_a].astype(F32)).astype(BF16)
        two_y(u).start()
        s2[u, part_b] = (s1[u, part_b].astype(F32) + f1[u, part_b].astype(F32)).astype(BF16)
        two_x(u).start()

    def finish(u):
        remote(s2.at[u], f2.at[u], t_send.at[u], u_recv.at[u], xn).wait_recv()
        at = pl.ds(pl.multiple_of(u * width, width), width)
        out_ref[at, :] = s2[u].astype(F32) + f2[u].astype(F32)

    def stage1(pos):
        def f(unit):
            row_copy(unit).wait_recv()
            s1[unit] = (acc[unit] + rbuf[unit].astype(F32)).astype(BF16)
            if pos[3] is None:
                begin(unit)
            else:
                z_copy(pos[3]).start()
        owned(pos, f)

    line = []

    def advance(pos):
        if pos is not None:
            stage0(pos)
        line.append(pos)
        n = len(line) - 1
        if n >= 2 and line[n - 2] is not None:
            stage1(line[n - 2])
        if n >= 4 and line[n - 4] is not None:
            owned(line[n - 4], turn)
        if n >= 6 and line[n - 6] is not None:
            owned(line[n - 6], finish)

    def half_copy(p, dev):
        return remote(half.at[p], half_r.at[p], p_send.at[p], h_recv.at[p], dev)

    true = c >= 0

    def arrive(t, kinds="rh"):
        for i in range(4):
            @pl.when(c == i)
            def _():
                for table, passed, send, on in ((FROM_RIGHT, PASS_LEFT, send_left, 1), (FROM_LEFT, PASS_RIGHT, send_right, 2)):
                    item = table[i][t - 1]
                    if item is None or item[0] not in kinds:
                        continue
                    if item[0] == "h":
                        half_copy(item[1], left if i == 2 else right).wait_recv()
                    else:
                        send(item[1], item[2]).wait_recv()
                        if i == on:
                            pass_piece(item[1], item[2], end).start()
                        for b, k in passed.get((i, t), []):
                            if b == i:
                                for p in LAST_ORDER:
                                    last_piece(c, p).start()
                            else:
                                send(b, k).start()

    def for_end(q):
        return (mid,) + end_chunk(q) + (q,)

    def part_for_end(q, first, last):
        @pl.when(mid)
        def _():
            product(*end_chunk(q), half_r, 2 * NCH + q, first, last)

    def positions(t):
        for table in (FROM_RIGHT, FROM_LEFT):
            items = [table[i][t - 1] for i in range(4)]
            ok = [1 if it is not None and it[0] == "r" else 0 for it in items]
            blocks = [it[1] if o else 0 for it, o in zip(items, ok)]
            chunks = [it[2] if o else 0 for it, o in zip(items, ok)]
            yield (pick(ok) == 1, pick(blocks), pick(chunks), None)

    arrive(1)
    for k in range(NCH):
        advance((true, c, k, None))

    @pl.when(c == 0)
    def _():
        for p in range(SPLIT):
            half_copy(p, right).start()

    @pl.when(c == 3)
    def _():
        for p in range(SPLIT):
            half_copy(p, left).start()

    for t in range(1, 7):
        if t > 1:
            arrive(t)
        for pos in positions(t):
            advance(pos)
        if t == 5:
            for q in range(5):
                part_for_end(q, 0, 1)
        if t == 6:
            for q in range(5):
                part_for_end(q, 1, 2)
            part_for_end(5, 0, 2)
    arrive(7, "h")

    @pl.when(mid)
    def _():
        for q in range(6):
            product(*end_chunk(q), half_r, 2 * NCH + q, 2, 3)
            to_mate(for_end(q))
        for q in range(6):
            stage1(for_end(q))
    arrive(7, "r")
    for pos in positions(7):
        advance(pos)

    @pl.when(mid)
    def _():
        product(*end_chunk(6), half_r, 2 * NCH + 6, 0, 3)
        to_mate(for_end(6))
        stage1(for_end(6))
    for _ in range(6):
        advance(None)

    own_last = (mid, 3 - c, NCH - 1, None)
    end_last = for_end(NREM - 1)
    at_end = jnp.logical_or(c == 0, c == 3)
    keeper = jnp.logical_or(jnp.logical_and(c == 0, r == 1), jnp.logical_and(c == 3, r == 0))

    def exchanged(u):
        both = s1.at[pl.ds(0, 2)]
        remote(both, both, t_send.at[u], t_recv.at[u], xn).wait_send()

    def sent(pos):
        @pl.when(pos[0])
        def _():
            unit = unit_at(pos)

            @pl.when(pos[1] // 2 != r)
            def _():
                row_copy(unit).wait_send()

            @pl.when(pos[1] // 2 == r)
            def _():
                if pos[3] is None:
                    exchanged(unit)
                else:
                    z_copy(pos[3]).wait_send()

    def settle():
        give_sig.wait_send()

        @pl.when(c > 0)
        def _():
            env_left(c).wait_send()

        @pl.when(c < 3)
        def _():
            env_right(c, 4).wait_send()
        for d in range(1, 4):
            @pl.when(c >= d)
            def _(b=c - d):
                @pl.when(c < 3)
                def _():
                    env_right(b).wait_send()
                env_x(b).wait_send()
                env_y(b).wait_send()

            @pl.when(c + d <= 3)
            def _(b=c + d):
                @pl.when(c > 0)
                def _():
                    env_left(b).wait_send()
                env_x(b).wait_send()
                env_y(b).wait_send()
        for i in range(4):
            @pl.when(c == i)
            def _():
                for b, k in FIRST_LEFT.get(i, []):
                    send_left(b, k).wait_send()
                for b, k in FIRST_RIGHT.get(i, []):
                    send_right(b, k, 4).wait_send()
                for passed, send in ((PASS_LEFT, send_left), (PASS_RIGHT, send_right)):
                    for (j, t), v in passed.items():
                        for b, k in v:
                            if j == i and b != i:
                                send(b, k).wait_send()
                if i in (0, 3):
                    for p in range(SPLIT):
                        half_copy(p, right if i == 0 else left).wait_send()
        for pos in line:
            if pos is not None:
                sent(pos)

    @pl.when(mid)
    def _():
        settle()

    def last_products(p):
        last_piece(3 - c, p).wait_recv()
        first, final = p == LAST_ORDER[0], p == LAST_ORDER[-1]
        if p == SPLIT:
            end_piece(NREM - 1).start()
        else:
            product(3 - c, NCH - 1, half_r, slot_at(end_last), p, p + 1)
        if final:
            to_mate(end_last)
        product(3 - c, NCH - 1, half, slot_at(own_last), p, p + 1, zero=first)
        if final:
            to_mate(own_last)

    @pl.when(mid)
    def _():
        for q in range(6):
            end_piece(q).wait_send()
            sent(for_end(q))
        for p in LAST_ORDER:
            last_products(p)
        stage1(end_last)
        stage1(own_last)
        owned(own_last, turn)
        owned(own_last, finish)
        end_piece(6).wait_send()
        end_piece(7).wait_send()
        sent(for_end(6))
        sent(end_last)
        sent(own_last)
        for p in LAST_ORDER:
            last_piece(c, p).wait_send()

    def end_part(q):
        pos = (at_end,) + end_chunk(q) + (None,)
        end_piece(q).wait_recv()
        product(pos[1], pos[2], half, slot_at(pos), SPLIT, SPLIT + 1, zero=True)
        to_mate(pos)

    def gather(q):
        u = end_unit(q)
        row_copy(u).wait_recv()
        z_copy(q).wait_recv()
        s1[u] = (acc[u] + rbuf[u].astype(F32) + zbuf[u].astype(F32)).astype(BF16)
        begin(u)

    @pl.when(at_end)
    def _():
        for q in range(NREM - 2):
            end_part(q)
        settle()

        @pl.when(keeper)
        def _():
            for n in range(NREM - 2 + 4):
                if n < NREM - 2:
                    gather(n)
                if 0 <= n - 2 < NREM - 2:
                    turn(end_unit(n - 2))
                if 0 <= n - 4:
                    finish(end_unit(n - 4))
            for q in range(NREM - 2):
                exchanged(end_unit(q))
        for q in (NREM - 2, NREM - 1):
            end_part(q)

        @pl.when(keeper)
        def _():
            for q in (NREM - 2, NREM - 1):
                gather(q)
                turn(end_unit(q))
                finish(end_unit(q))
            for q in (NREM - 2, NREM - 1):
                exchanged(end_unit(q))

        @pl.when(jnp.logical_not(keeper))
        def _():
            for q in range(NREM):
                row_copy(end_unit(q)).wait_send()


def fused(rho_sites, sigma_sites, environment):
    _, pairs, rows, cols = rho_sites.shape
    width = cols // NCH
    units = 2 * NCH
    sem = pltpu.SemaphoreType.DMA
    piece = (units + NREM, width, cols)
    pair = (units, width, cols)
    return pl.pallas_call(
        kernel,
        out_shape=pltpu.VMEM(environment.shape, F32),
        in_specs=[pl.BlockSpec(memory_space=pl.ANY)] * 3,
        out_specs=pl.BlockSpec(memory_space=pltpu.VMEM),
        scratch_shapes=[
            pltpu.VMEM((4, NCH, pairs, rows, width), BF16),
            pltpu.VMEM((pairs, 2 * rows, cols), BF16),
            pltpu.VMEM((rows, cols), F32),
            pltpu.VMEM((4, rows, cols), BF16),
            pltpu.VMEM((pairs, rows, cols), BF16),
            pltpu.VMEM((pairs, rows, cols), BF16),
            pltpu.VMEM((units + NREM + 1, width, cols), F32),
            pltpu.VMEM(piece, BF16), pltpu.VMEM(piece, BF16), pltpu.VMEM(piece, BF16),
            pltpu.VMEM(pair, BF16), pltpu.VMEM(pair, BF16), pltpu.VMEM(pair, BF16), pltpu.VMEM(pair, BF16),
            sem((5, NCH)), sem((4, NCH)), sem((4,)), sem((4,)), sem((SPLIT,)),
            sem((5 + NCH,)), sem, sem,
            sem((5,)), sem((4,)), sem((4,)), sem((4,)), sem((4,)), sem((4,)),
            sem((units + NREM,)), sem((units + NREM,)),
            sem((units,)), sem((units,)), sem((units,)),
        ],
        compiler_params=pltpu.CompilerParams(
            collective_id=0, has_side_effects=True, vmem_limit_bytes=58 * 1024 * 1024
        ),
    )(rho_sites, sigma_sites, environment)


def plain(rho_sites, sigma_sites, environment):
    env_whole = lax.all_gather(environment.astype(BF16), "col", axis=1, tiled=True)
    half = jnp.einsum(
        "ik,pkl->pil",
        env_whole,
        lax.all_gather(sigma_sites[0], "row", axis=1, tiled=True),
        preferred_element_type=F32,
    ).astype(BF16)
    partial_env = jnp.einsum(
        "pij,pil->jl",
        lax.all_gather(rho_sites[0], "col", axis=2, tiled=True),
        half,
        preferred_element_type=F32,
    )
    row_part = lax.psum_scatter(partial_env, "row", scatter_dimension=0, tiled=True)
    return lax.psum(row_part, "phys")


def solution(mesh):
    placed = (P(None, "phys", "row", "col"), P(None, "phys", "row", "col"), P("row", "col"))
    sizes = (mesh.shape["phys"], mesh.shape["row"], mesh.shape["col"])
    body = fused if sizes == (4, 2, 4) else plain
    return jax.shard_map(body, mesh=mesh, in_specs=placed, out_specs=P("row", "col"), check_vma=False)
```

```python
import functools

import jax
import jax.numpy as jnp
from jax import lax
from jax.experimental import pallas as pl
from jax.experimental.pallas import tpu as pltpu
from jax.sharding import PartitionSpec as P

MESH = pl.DeviceIdType.MESH
NCH = 4
FROM_RIGHT = {
    0: [("r", 1, k) for k in range(4)] + [None] * 3,
    1: [("r", 2, 0), ("r", 2, 1), ("r", 2, 2), ("r", 3, 0), ("r", 3, 1), ("r", 3, 2), ("r", 3, 3)],
    2: [("r", 3, k) for k in range(4)] + [("h", p) for p in range(3)],
    3: [None] * 7,
}


def mirror(item):
    if item is None or item[0] == "h":
        return item
    return ("r", 3 - item[1], item[2])


FROM_LEFT = {3 - c: [mirror(i) for i in seq] for c, seq in FROM_RIGHT.items()}
PASS_LEFT = {(2, 1): [(3, 0)], (2, 2): [(3, 1)], (2, 3): [(3, 2)], (2, 4): [(3, 3), (2, 3)]}
PASS_RIGHT = {(3 - c, t): [(3 - b, k) for b, k in v] for (c, t), v in PASS_LEFT.items()}
FIRST_LEFT = {1: [(1, k) for k in range(4)], 2: [(2, 0), (2, 1), (2, 2)], 3: [(3, k) for k in range(4)]}
FIRST_RIGHT = {3 - c: [(3 - b, k) for b, k in v] for c, v in FIRST_LEFT.items()}
FOR_END = [(2, 0), (2, 1), (2, 2), (3, 0), (3, 1), (3, 2), (3, 3), (2, 3)]
NREM = len(FOR_END)
SPLIT = 3
LAST = 7
PARTS = 4
F32 = jnp.float32
BF16 = jnp.bfloat16


def kernel(rho_ref, sig_ref, env_ref, out_ref,
           rho_g, sig, env_f, env_g, half, half_r, acc, psend, rbuf, s1, f1, s2, f2, zbuf, pk_far, pk_mid,
           r_send, r_recv, p_send, l_recv, h_recv, loc, sg_send, sg_recv,
           e_send, e_recv, ex_send, ex_recv, ey_send, ey_recv,
           row_send, row_recv, t_send, t_recv, u_recv):
    ph = lax.axis_index("phys")
    r = lax.axis_index("row")
    c = lax.axis_index("col")
    width = rho_g.shape[-1]
    rows = rho_g.shape[3]
    quarter = rows // 4
    group = rows // PARTS
    lanes = width // PARTS
    ind3 = c // 3
    ind2 = c // 2 - ind3
    ind0 = (3 - c) // 3
    ind1 = 1 - ind0 - ind2 - ind3
    inds = (ind0, ind1, ind2, ind3)

    def pick(values):
        total = 0
        for i, v in zip(inds, values):
            total = total + i * v
        return total

    mate = {"row": 1 - r}
    xn = {"phys": ph + 1 - 2 * (ph % 2)}
    yn = {"phys": (ph + 2) % 4}
    left = {"col": c - 1}
    right = {"col": c + 1}
    mid = jnp.logical_and(c > 0, c < 3)
    middle = {"col": 3 - c}
    end = {"col": 3 * (c // 2)}

    def remote(src, dst, ss, rs, dev):
        return pltpu.make_async_remote_copy(src_ref=src, dst_ref=dst, send_sem=ss, recv_sem=rs,
                                            device_id=dev, device_id_type=MESH)

    env_parts = [pl.ds(pl.multiple_of((ph + j) % 4 * quarter, quarter), quarter) for j in range(4)]
    load_env = [pltpu.make_async_copy(env_ref.at[at], env_f.at[at], loc.at[1 + NCH + j]) for j, at in enumerate(env_parts)]
    load_env[0].start()
    load_rho = [pltpu.make_async_copy(rho_ref.at[0, :, :, pl.ds(k * width, width)], rho_g.at[c, k], loc.at[k]) for k in range(NCH)]
    for cp in load_rho:
        cp.start()
    for cp in load_env[1:]:
        cp.start()
    my_rows = pl.ds(pl.multiple_of(r * rows, rows), rows)
    load_sig = pltpu.make_async_copy(sig_ref.at[0], sig.at[:, my_rows, :], loc.at[NCH])
    load_sig.start()

    barrier = pltpu.get_barrier_semaphore()
    for dev in (mate, xn, yn):
        pl.semaphore_signal(barrier, inc=1, device_id=dev, device_id_type=MESH)

    @pl.when(c > 0)
    def _():
        pl.semaphore_signal(barrier, inc=1, device_id=left, device_id_type=MESH)

    @pl.when(c < 3)
    def _():
        pl.semaphore_signal(barrier, inc=1, device_id=right, device_id_type=MESH)

    def cast_env(j):
        load_env[j].wait()
        env_g[c, env_parts[j]] = env_f[env_parts[j]].astype(BF16)

    cast_env(0)
    pl.semaphore_wait(barrier, 3 + pick((1, 2, 2, 1)))

    q_rows = env_parts[0]
    h_rows = pl.ds(pl.multiple_of((ph // 2) * 2 * quarter, 2 * quarter), 2 * quarter)

    def env_left(b):
        return remote(env_g.at[b, q_rows], env_g.at[b, q_rows], e_send.at[b], e_recv.at[b], left)

    def env_right(b, slot=None):
        slot = b if slot is None else slot
        return remote(env_g.at[b, q_rows], env_g.at[b, q_rows], e_send.at[slot], e_recv.at[b], right)

    def env_x(b):
        return remote(env_g.at[b, q_rows], env_g.at[b, q_rows], ex_send.at[b], ex_recv.at[b], xn)

    def env_y(b):
        return remote(env_g.at[b, h_rows], env_g.at[b, h_rows], ey_send.at[b], ey_recv.at[b], yn)

    def send_left(b, k):
        return remote(rho_g.at[b, k], rho_g.at[b, k], r_send.at[b, k], r_recv.at[b, k], left)

    def send_right(b, k, slot=None):
        slot = b if slot is None else slot
        return remote(rho_g.at[b, k], rho_g.at[b, k], r_send.at[slot, k], r_recv.at[b, k], right)

    def first_piece(p):
        at = rho_g.at[c, 0, p]
        remote(at, at, r_send.at[c, 0], r_recv.at[c, 0], left).start()
        remote(at, at, r_send.at[4, 0], r_recv.at[c, 0], right).start()

    def pass_piece(b, k, dev):
        at = rho_g.at[b, k, SPLIT]
        return remote(at, at, r_send.at[b, k], r_recv.at[b, k], dev)

    def last_piece(n):
        if n == 0:
            src, dst = pk_far.at[0], pk_far.at[1]
        elif n < PARTS:
            src, dst = pk_mid.at[0, n - 1], pk_mid.at[1, n - 1]
        else:
            src, dst = pk_mid.at[0, PARTS - 1, n - PARTS], pk_mid.at[1, PARTS - 1, n - PARTS]
        return remote(src, dst, p_send.at[n], l_recv.at[n], middle)

    @pl.when(c > 0)
    def _():
        env_left(c).start()

    @pl.when(c < 3)
    def _():
        env_right(c, 4).start()

    give_sig = remote(sig_ref.at[0], sig.at[:, my_rows, :], sg_send, sg_recv, mate)
    load_rho[0].wait()

    @pl.when(mid)
    def _():
        first_piece(0)
    give_sig.start()
    for j in range(1, 4):
        cast_env(j)

    def first_sends(i, k):
        for b, kk in FIRST_LEFT.get(i, []):
            if kk == k:
                send_left(b, k).start()
        for b, kk in FIRST_RIGHT.get(i, []):
            if kk == k:
                send_right(b, k, 4).start()

    for k in range(NCH):
        if k:
            load_rho[k].wait()
        for i in (0, 3):
            @pl.when(c == i)
            def _():
                first_sends(i, k)

    for d in range(1, 4):
        @pl.when(c >= d)
        def _(b=c - d):
            env_right(b).wait_recv()

            @pl.when(c < 3)
            def _():
                env_right(b).start()
            env_x(b).start()

        @pl.when(c + d <= 3)
        def _(b=c + d):
            env_left(b).wait_recv()

            @pl.when(c > 0)
            def _():
                env_left(b).start()
            env_x(b).start()
        if d == 1:
            @pl.when(mid)
            def _():
                first_piece(1)
        if d == 2:
            @pl.when(mid)
            def _():
                first_piece(2)
                first_piece(3)
            for i in (1, 2):
                @pl.when(c == i)
                def _():
                    for k in range(1, NCH):
                        first_sends(i, k)

    def others(f):
        for d in range(1, 4):
            @pl.when(c >= d)
            def _(b=c - d):
                f(b)

            @pl.when(c + d <= 3)
            def _(b=c + d):
                f(b)

    def env_y_of(b):
        env_x(b).wait_recv()
        env_y(b).start()
    others(env_y_of)
    others(lambda b: env_y(b).wait_recv())
    load_sig.wait()
    give_sig.wait_recv()

    tile = min(256, rows)

    @pl.loop(0, 4)
    def _(p):
        @pl.loop(0, rows // tile)
        def _(m):
            here = pl.ds(pl.multiple_of(m * tile, tile), tile)
            total = jnp.dot(env_g[0, here, :], sig[p, pl.ds(0, 512), :], preferred_element_type=F32)
            for b in range(1, 4):
                total += jnp.dot(env_g[b, here, :], sig[p, pl.ds(b * 512, 512), :], preferred_element_type=F32)
            half[p, here, :] = total.astype(BF16)

    def unit_of(b, k):
        return (b % 2) * NCH + k

    def product(b, k, other, unit, first=0, last=4, zero=None):
        if zero or (zero is None and first == 0):
            acc[unit] = jnp.zeros_like(acc.at[unit])

        @pl.loop(first, last)
        def _(p):
            acc[unit] += lax.dot_general(rho_g[b, k, p], other[p], (((0,), (0,)), ((), ())),
                                         preferred_element_type=F32)

    def row_copy(unit):
        return remote(psend.at[unit], rbuf.at[unit], row_send.at[unit], row_recv.at[unit], mate)

    whole = (0, width)
    main = (0, width - lanes)
    rest = (width - lanes, lanes)

    def halves(part):
        lo, n = part
        return pl.ds(lo, n // 2), pl.ds(lo + n // 2, n // 2)

    def lane_of(u, part):
        return 2 * NCH if part is rest else u

    def one_x(u, part):
        at, i = halves(part)[0], lane_of(u, part)
        return remote(s1.at[u, at], f1.at[u, at], t_send.at[i], t_recv.at[i], xn)

    def one_y(u, part):
        at, i = halves(part)[1], lane_of(u, part)
        return remote(s1.at[u, at], f1.at[u, at], t_send.at[i], t_recv.at[i], yn)

    def two_y(u, part):
        at, i = halves(part)[0], lane_of(u, part)
        return remote(s2.at[u, at], f2.at[u, at], t_send.at[i], u_recv.at[i], yn)

    def two_x(u, part):
        at, i = halves(part)[1], lane_of(u, part)
        return remote(s2.at[u, at], f2.at[u, at], t_send.at[i], u_recv.at[i], xn)

    def end_chunk(q):
        b, k = FOR_END[q]
        return pick((b, b, 3 - b, 3 - b)), k

    def end_unit(q):
        b, k = FOR_END[q]
        there, mirrored = unit_of(b, k), unit_of(3 - b, k)
        return pick((there, there, mirrored, mirrored))

    def z_copy(q):
        return remote(s1.at[2 * NCH + q], zbuf.at[end_unit(q)], row_send.at[2 * NCH + q], row_recv.at[2 * NCH + q], end)

    def end_piece(q):
        return pass_piece(*end_chunk(q), end)

    def unit_at(pos):
        _, b, k, q = pos
        return unit_of(b, k) if q is None else 2 * NCH + q

    def slot_at(pos):
        _, b, k, q = pos
        if q is not None:
            return 2 * NCH + q
        owner = b // 2
        own = 1 - (owner + r - 2 * owner * r)
        return own * unit_of(b, k) + (1 - own) * (2 * NCH + NREM)

    def to_mate(pos):
        @pl.when(pos[1] // 2 != r)
        def _():
            psend[unit_at(pos)] = acc[slot_at(pos)].astype(BF16)
            row_copy(unit_at(pos)).start()

    def stage0(pos, first=0):
        valid, b, k, q = pos

        @pl.when(valid)
        def _():
            product(b, k, half if q is None else half_r, slot_at(pos), first)
            to_mate(pos)

    def owned(pos, f):
        valid, b, k, q = pos

        @pl.when(jnp.logical_and(valid, b // 2 == r))
        def _():
            f(unit_at(pos))

    def begin(u, part=whole):
        one_x(u, part).start()
        one_y(u, part).start()

    def turn(u, part=whole):
        at, i = pl.ds(*part), lane_of(u, part)
        remote(s1.at[u, at], f1.at[u, at], t_send.at[i], t_recv.at[i], xn).wait_recv()
        for at, copy in zip(halves(part), (two_y, two_x)):
            s2[u, at] = (s1[u, at].astype(F32) + f1[u, at].astype(F32)).astype(BF16)
            copy(u, part).start()

    def finish(u, part=whole):
        at, i = pl.ds(*part), lane_of(u, part)
        remote(s2.at[u, at], f2.at[u, at], t_send.at[i], u_recv.at[i], xn).wait_recv()
        to = pl.ds(pl.multiple_of(u * width, width) + part[0], part[1])
        out_ref[to, :] = s2[u, at].astype(F32) + f2[u, at].astype(F32)

    def stage1(pos):
        def f(unit):
            row_copy(unit).wait_recv()
            s1[unit] = (acc[unit] + rbuf[unit].astype(F32)).astype(BF16)
            if pos[3] is None:
                begin(unit)
            else:
                z_copy(pos[3]).start()
        owned(pos, f)

    line = []

    def advance(pos):
        if pos is not None:
            stage0(pos)
        line.append(pos)
        n = len(line) - 1
        if n >= 2 and line[n - 2] is not None:
            stage1(line[n - 2])
        if n >= 4 and line[n - 4] is not None:
            owned(line[n - 4], turn)
        if n >= 6 and line[n - 6] is not None:
            owned(line[n - 6], finish)

    def half_copy(p, dev):
        return remote(half.at[p], half_r.at[p], p_send.at[p], h_recv.at[p], dev)

    true = c >= 0

    def arrive(t, kinds="rh"):
        for i in range(4):
            @pl.when(c == i)
            def _():
                for table, passed, send, on in ((FROM_RIGHT, PASS_LEFT, send_left, 1), (FROM_LEFT, PASS_RIGHT, send_right, 2)):
                    item = table[i][t - 1]
                    if item is None or item[0] not in kinds:
                        continue
                    if item[0] == "h":
                        half_copy(item[1], left if i == 2 else right).wait_recv()
                    else:
                        send(item[1], item[2]).wait_recv()
                        if i == on:
                            pass_piece(item[1], item[2], end).start()
                        for b, k in passed.get((i, t), []):
                            if b == i:
                                for n in range(LAST):
                                    last_piece(n).start()
                            else:
                                send(b, k).start()

    def for_end(q):
        return (mid,) + end_chunk(q) + (q,)

    def part_for_end(q, first, last):
        @pl.when(mid)
        def _():
            product(*end_chunk(q), half_r, 2 * NCH + q, first, last)

    def positions(t):
        for table in (FROM_RIGHT, FROM_LEFT):
            items = [table[i][t - 1] for i in range(4)]
            ok = [1 if it is not None and it[0] == "r" else 0 for it in items]
            blocks = [it[1] if o else 0 for it, o in zip(items, ok)]
            chunks = [it[2] if o else 0 for it, o in zip(items, ok)]
            yield (pick(ok) == 1, pick(blocks), pick(chunks), None)

    arrive(1)
    for k in range(NCH):
        advance((true, c, k, None))

    lane = lax.broadcasted_iota(jnp.int32, (group, width), 1) // lanes

    def repacked(p, j):
        total = None
        for g in range(PARTS):
            x = rho_g[c, NCH - 1, p, pl.ds(g * group, group), :].astype(F32)
            shift = (g - j) * lanes % width
            if shift:
                x = pltpu.roll(x, shift, 1)
            total = x if g == 0 else jnp.where(lane == g, x, total)
        return total.astype(BF16)

    @pl.when(mid)
    def _():
        @pl.loop(0, SPLIT)
        def _(p):
            for j in range(PARTS):
                pk_mid[0, j, p] = repacked(p, j)
        for j in range(PARTS):
            pk_far[0, j] = repacked(SPLIT, j)

    def packed_product(lhs, other, p, slot, j):
        total = 0
        for g in range(PARTS):
            part = lax.dot_general(lhs[...], other[p, pl.ds(g * group, group), :], (((0,), (0,)), ((), ())),
                                   preferred_element_type=F32)
            total = total + part[g * lanes:(g + 1) * lanes]
        at = pl.ds(pl.multiple_of(j * lanes, lanes), lanes)
        acc[slot, at] += total

    @pl.when(c == 0)
    def _():
        for p in range(SPLIT):
            half_copy(p, right).start()

    @pl.when(c == 3)
    def _():
        for p in range(SPLIT):
            half_copy(p, left).start()

    for t in range(1, 7):
        if t > 1:
            arrive(t)
        for pos in positions(t):
            advance(pos)
        if t == 5:
            for q in range(5):
                part_for_end(q, 0, 1)
        if t == 6:
            for q in range(5):
                part_for_end(q, 1, 2)
            part_for_end(5, 0, 2)
    arrive(7, "h")

    @pl.when(mid)
    def _():
        for q in range(6):
            product(*end_chunk(q), half_r, 2 * NCH + q, 2, 3)
            to_mate(for_end(q))
        for q in range(6):
            stage1(for_end(q))
    arrive(7, "r")
    for pos in positions(7):
        advance(pos)

    @pl.when(mid)
    def _():
        product(*end_chunk(6), half_r, 2 * NCH + 6, 0, 3)
        to_mate(for_end(6))
        stage1(for_end(6))
    for _ in range(6):
        advance(None)

    own_last = (mid, 3 - c, NCH - 1, None)
    end_last = for_end(NREM - 1)
    at_end = jnp.logical_or(c == 0, c == 3)
    keeper = jnp.logical_or(jnp.logical_and(c == 0, r == 1), jnp.logical_and(c == 3, r == 0))

    def exchanged(u, part=whole):
        both, i = s1.at[pl.ds(0, 2), pl.ds(*part)], lane_of(u, part)
        remote(both, both, t_send.at[i], t_recv.at[i], xn).wait_send()

    def sent(pos):
        @pl.when(pos[0])
        def _():
            unit = unit_at(pos)

            @pl.when(pos[1] // 2 != r)
            def _():
                row_copy(unit).wait_send()

            @pl.when(pos[1] // 2 == r)
            def _():
                if pos[3] is None:
                    exchanged(unit)
                else:
                    z_copy(pos[3]).wait_send()

    def settle():
        give_sig.wait_send()

        @pl.when(c > 0)
        def _():
            env_left(c).wait_send()

        @pl.when(c < 3)
        def _():
            env_right(c, 4).wait_send()
        for d in range(1, 4):
            @pl.when(c >= d)
            def _(b=c - d):
                @pl.when(c < 3)
                def _():
                    env_right(b).wait_send()
                env_x(b).wait_send()
                env_y(b).wait_send()

            @pl.when(c + d <= 3)
            def _(b=c + d):
                @pl.when(c > 0)
                def _():
                    env_left(b).wait_send()
                env_x(b).wait_send()
                env_y(b).wait_send()
        for i in range(4):
            @pl.when(c == i)
            def _():
                for b, k in FIRST_LEFT.get(i, []):
                    send_left(b, k).wait_send()
                for b, k in FIRST_RIGHT.get(i, []):
                    send_right(b, k, 4).wait_send()
                for passed, send in ((PASS_LEFT, send_left), (PASS_RIGHT, send_right)):
                    for (j, t), v in passed.items():
                        for b, k in v:
                            if j == i and b != i:
                                send(b, k).wait_send()
                if i in (0, 3):
                    for p in range(SPLIT):
                        half_copy(p, right if i == 0 else left).wait_send()
        for pos in line:
            if pos is not None:
                sent(pos)

    @pl.when(mid)
    def _():
        settle()

    def far_piece():
        return remote(pk_far.at[1], pk_far.at[1], r_send.at[3 - c, NCH - 1], r_recv.at[end_chunk(NREM - 1)[0], NCH - 1], end)

    def row_index(pos, part):
        if part is main:
            return unit_at(pos)
        return 2 * NCH + NREM + (0 if pos[3] is not None else 1)

    def row_part(pos, part):
        u, at, i = unit_at(pos), pl.ds(*part), row_index(pos, part)
        return remote(psend.at[u, at], rbuf.at[u, at], row_send.at[i], row_recv.at[i], mate)

    def z_part(part):
        at, i = pl.ds(*part), 2 * NCH + NREM - 1 if part is main else 2 * NCH + NREM
        q = NREM - 1
        return remote(s1.at[2 * NCH + q, at], zbuf.at[end_unit(q), at], row_send.at[i], row_recv.at[i], end)

    def to_mate_part(pos, part):
        @pl.when(pos[1] // 2 != r)
        def _():
            at = pl.ds(*part)
            psend[unit_at(pos), at] = acc[slot_at(pos), at].astype(BF16)
            row_part(pos, part).start()

    def row_sum(pos, part):
        at = pl.ds(*part)

        def f(unit):
            row_part(pos, part).wait_recv()
            s1[unit, at] = (acc[unit, at] + rbuf[unit, at].astype(F32)).astype(BF16)
            if pos[3] is None:
                begin(unit, part)
            else:
                z_part(part).start()
        owned(pos, f)

    def last_products(n):
        last_piece(n).wait_recv()
        if n == 0:
            far_piece().start()

            @pl.loop(0, PARTS)
            def _(j):
                packed_product(pk_far.at[1, j], half, SPLIT, slot_at(own_last), j)
        elif n < PARTS:
            @pl.loop(0, SPLIT)
            def _(p):
                packed_product(pk_mid.at[1, n - 1, p], half_r, p, slot_at(end_last), n - 1)
                packed_product(pk_mid.at[1, n - 1, p], half, p, slot_at(own_last), n - 1)
        else:
            p = n - PARTS
            packed_product(pk_mid.at[1, PARTS - 1, p], half_r, p, slot_at(end_last), PARTS - 1)
            if n == LAST - 1:
                to_mate_part(end_last, rest)
            packed_product(pk_mid.at[1, PARTS - 1, p], half, p, slot_at(own_last), PARTS - 1)
            if n == LAST - 1:
                to_mate_part(own_last, rest)

    @pl.when(mid)
    def _():
        for q in range(6):
            end_piece(q).wait_send()
            sent(for_end(q))
        for pos in (end_last, own_last):
            acc[slot_at(pos)] = jnp.zeros_like(acc.at[0])
        for n in range(PARTS):
            last_products(n)
        to_mate_part(end_last, main)
        to_mate_part(own_last, main)
        last_products(PARTS)
        row_sum(end_last, main)
        row_sum(own_last, main)
        for n in range(PARTS + 1, LAST):
            last_products(n)
        row_sum(end_last, rest)
        row_sum(own_last, rest)
        for part in (main, rest):
            owned(own_last, lambda u: turn(u, part))
        for part in (main, rest):
            owned(own_last, lambda u: finish(u, part))
        end_piece(6).wait_send()
        far_piece().wait_send()
        sent(for_end(6))
        for pos in (end_last, own_last):
            @pl.when(pos[1] // 2 != r)
            def _():
                for part in (main, rest):
                    row_part(pos, part).wait_send()

            @pl.when(pos[1] // 2 == r)
            def _():
                for part in (main, rest):
                    if pos[3] is None:
                        exchanged(unit_at(pos), part)
                    else:
                        z_part(part).wait_send()
        for n in range(LAST):
            last_piece(n).wait_send()

    def end_position(q):
        return (at_end,) + end_chunk(q) + (None,)

    def end_part(q):
        pos = end_position(q)
        if q < NREM - 1:
            end_piece(q).wait_recv()
            product(pos[1], pos[2], half, slot_at(pos), SPLIT, SPLIT + 1, zero=True)
        else:
            far_piece().wait_recv()
            acc[slot_at(pos)] = jnp.zeros_like(acc.at[0])

            @pl.loop(0, PARTS)
            def _(j):
                packed_product(pk_far.at[1, j], half, SPLIT, slot_at(pos), j)
        to_mate(pos)

    def gather(q, part=whole):
        u, at = end_unit(q), pl.ds(*part)
        if part is not rest:
            row_copy(u).wait_recv()
        if part is whole:
            z_copy(q).wait_recv()
        else:
            z_part(part).wait_recv()
        s1[u, at] = (acc[u, at] + rbuf[u, at].astype(F32) + zbuf[u, at].astype(F32)).astype(BF16)
        begin(u, part)

    @pl.when(at_end)
    def _():
        for q in range(NREM - 2):
            end_part(q)
        settle()

        @pl.when(keeper)
        def _():
            for n in range(NREM - 2 + 4):
                if n < NREM - 2:
                    gather(n)
                if 0 <= n - 2 < NREM - 2:
                    turn(end_unit(n - 2))
                if 0 <= n - 4:
                    finish(end_unit(n - 4))
            for q in range(NREM - 2):
                exchanged(end_unit(q))
        before, last = NREM - 2, NREM - 1
        end_part(before)

        @pl.when(keeper)
        def _():
            gather(before)
        end_part(last)

        @pl.when(keeper)
        def _():
            turn(end_unit(before))
            gather(last, main)
            gather(last, rest)
            for part in (main, rest):
                turn(end_unit(last), part)
            finish(end_unit(before))
            for part in (main, rest):
                finish(end_unit(last), part)
            exchanged(end_unit(before))
            for part in (main, rest):
                exchanged(end_unit(last), part)

        @pl.when(jnp.logical_not(keeper))
        def _():
            for q in range(NREM):
                row_copy(end_unit(q)).wait_send()


def fused(rho_sites, sigma_sites, environment):
    _, pairs, rows, cols = rho_sites.shape
    width = cols // NCH
    units = 2 * NCH
    sem = pltpu.SemaphoreType.DMA
    piece = (units + NREM, width, cols)
    pair = (units, width, cols)
    return pl.pallas_call(
        kernel,
        out_shape=pltpu.VMEM(environment.shape, F32),
        in_specs=[pl.BlockSpec(memory_space=pl.ANY)] * 3,
        out_specs=pl.BlockSpec(memory_space=pltpu.VMEM),
        scratch_shapes=[
            pltpu.VMEM((4, NCH, pairs, rows, width), BF16),
            pltpu.VMEM((pairs, 2 * rows, cols), BF16),
            pltpu.VMEM((rows, cols), F32),
            pltpu.VMEM((4, rows, cols), BF16),
            pltpu.VMEM((pairs, rows, cols), BF16),
            pltpu.VMEM((pairs, rows, cols), BF16),
            pltpu.VMEM((units + NREM + 1, width, cols), F32),
            pltpu.VMEM(piece, BF16), pltpu.VMEM(piece, BF16), pltpu.VMEM(piece, BF16),
            pltpu.VMEM(pair, BF16), pltpu.VMEM(pair, BF16), pltpu.VMEM(pair, BF16), pltpu.VMEM(pair, BF16),
            pltpu.VMEM((2, PARTS, rows // PARTS, width), BF16),
            pltpu.VMEM((2, PARTS, SPLIT, rows // PARTS, width), BF16),
            sem((5, NCH)), sem((4, NCH)), sem((LAST,)), sem((LAST,)), sem((SPLIT,)),
            sem((5 + NCH,)), sem, sem,
            sem((5,)), sem((4,)), sem((4,)), sem((4,)), sem((4,)), sem((4,)),
            sem((units + NREM + 2,)), sem((units + NREM + 2,)),
            sem((units + 1,)), sem((units + 1,)), sem((units + 1,)),
        ],
        compiler_params=pltpu.CompilerParams(
            collective_id=0, has_side_effects=True, vmem_limit_bytes=58 * 1024 * 1024
        ),
    )(rho_sites, sigma_sites, environment)


def plain(rho_sites, sigma_sites, environment):
    env_whole = lax.all_gather(environment.astype(BF16), "col", axis=1, tiled=True)
    half = jnp.einsum(
        "ik,pkl->pil",
        env_whole,
        lax.all_gather(sigma_sites[0], "row", axis=1, tiled=True),
        preferred_element_type=F32,
    ).astype(BF16)
    partial_env = jnp.einsum(
        "pij,pil->jl",
        lax.all_gather(rho_sites[0], "col", axis=2, tiled=True),
        half,
        preferred_element_type=F32,
    )
    row_part = lax.psum_scatter(partial_env, "row", scatter_dimension=0, tiled=True)
    return lax.psum(row_part, "phys")


def solution(mesh):
    placed = (P(None, "phys", "row", "col"), P(None, "phys", "row", "col"), P("row", "col"))
    sizes = (mesh.shape["phys"], mesh.shape["row"], mesh.shape["col"])
    body = fused if sizes == (4, 2, 4) else plain
    return jax.shard_map(body, mesh=mesh, in_specs=placed, out_specs=P("row", "col"), check_vma=False)
```
